256 devices in a mesh: section: 8 (over z), ctx: 16 (over y, x_hi, core), tp: 2 (over x_lo).
Axes of the slice: x: 4 (x_hi: 2, x_lo: 2; x = x_hi * 2 + x_lo), y: 4, z: 8, core: 2. Of those that a mesh axis runs over, the one named last changes fastest.
Arguments:
- x_in: bfloat16 [2, 4096, 2688], P(None, ('ctx', 'tp')), may hold values from -180 to 180
- norm_gain: bfloat16 [8, 2688], P('section'), may hold values from 0.099609375 to 1.8984375
- w_query: bfloat16 [8, 2688, 2048], P('section', None, 'tp'), may hold values from -1 to 1
- w_key: bfloat16 [8, 2688, 1024], P('section', 'ctx', 'tp'), may hold values from -3 to 3
- value_projection: bfloat16 [8, 2688, 1024], P('section', 'ctx', 'tp'), may hold values from -0.125 to 0.125
- w_out: bfloat16 [8, 2048, 2688], P('section', 'tp', 'ctx'), may hold values from -0.125 to 0.125
- doc_ids: int32 [2, 32], replicated, may hold values from 0 to 7, never falling along the last dimension, each value on 1 to 6 neighbouring positions
Outputs:
- layer_out: bfloat16 [8, 2, 4096, 2688], P('section', None, ('ctx', 'tp'))
The draws below stay inside these ranges and needn't reach their ends.
Inputs may be any that keep to these rules, and one draw needn't show every extreme that they name: Along each row doc_ids never falls, so each document covers whole consecutive blocks of 128 tokens.
All inputs are finite; a program needn't handle non-finite values.
Results may differ from the reference program's by a relative error of at most 0.018.
Values may be sent and summed in bfloat16 or wider, within the bound.
A program may use at most 128 MiB of HBM per device.

```python
import math
import jax
import jax.numpy as jnp
import numpy as np
from jax import lax

MODEL_DIM = 2688
QUERY_HEADS = 16
KEY_VALUE_HEADS = 8
HEAD_SIZE = 128
WINDOW = 1024
BLOCK = 128
MICRO = 2
TOK_DEV = 256
PACKED_TOKENS = 4096
NBLK = 32
LAYER_COUNT = 8


def query_rotary_base(key):
    random_noise = jax.random.normal(jax.random.fold_in(key, 11), (LAYER_COUNT, MODEL_DIM, QUERY_HEADS * HEAD_SIZE), jnp.float32)
    return jnp.clip(random_noise, -5.0, 5.0) * MODEL_DIM ** (-0.5)


def draw_w_query(key, part):
    return query_rotary_base(key).astype(jnp.bfloat16)


def draw_w_key(key, part):
    random_noise = jax.random.normal(jax.random.fold_in(key, 12), (LAYER_COUNT, MODEL_DIM, KEY_VALUE_HEADS * HEAD_SIZE), jnp.float32)
    layer_result = jnp.clip(random_noise, -5.0, 5.0) * MODEL_DIM ** (-0.5)
    return layer_result.astype(jnp.bfloat16)


def draw_x_in(key, part):
    random_noise = jnp.clip(jax.random.normal(jax.random.fold_in(key, 21), (MICRO, PACKED_TOKENS, MODEL_DIM), jnp.float32), -5.0, 5.0)
    layer_result = random_noise
    return layer_result.astype(jnp.bfloat16)


def block_scale(key, extent, pieces, smallest, high):
    def one(dim, parts):
        heights = jax.random.uniform(jax.random.fold_in(jax.random.fold_in(key, 6), dim), (parts,), jnp.float32, smallest / len(pieces), high / len(pieces))
        return jnp.repeat(jnp.exp(heights), extent[dim] // parts).reshape((-1,) + (1,) * (len(extent) - dim - 1))

    factor_of = one(*pieces[0])
    for cut in pieces[1:]:
        factor_of = factor_of * one(*cut)
    return factor_of


def profile(amount, total, limit, lean):
    loads = [(1 << 20) // math.isqrt(grade ** lean) + 1 for grade in range(2, amount + 1)]
    rest, counts = total - limit - (amount - 1), [1] * (amount - 1)
    while rest > 0:
        free = [i for i in range(amount - 1) if counts[i] < limit]
        pool, left = sum([loads[i] for i in free]), rest
        for i in free:
            more = min(limit - counts[i], max(1, left * loads[i] // pool), rest)
            counts[i] = counts[i] + more
            rest = rest - more
    return np.array([limit] + counts)


def uneven_parts(key, count, total, most, slope):
    if count == 2:
        one = jax.random.randint(key, (), max(1, total - most), min(most, total - 1) + 1)
        return jnp.stack([one, total - one])
    sizes = jnp.asarray(profile(count, total, most, slope), jnp.int32)
    twos = (count - 1) // 2
    giver, taker = sizes[1:1 + 2 * twos:2], sizes[2:2 + 2 * twos:2]
    margin = jnp.minimum(giver - 1, most - taker)
    moved = jax.random.randint(jax.random.fold_in(key, 1), (twos,), 0, 1 << 20) % (margin + 1)
    sizes = sizes.at[1:1 + 2 * twos:2].set(giver - moved).at[2:2 + 2 * twos:2].set(taker + moved)
    return sizes[jax.random.permutation(jax.random.fold_in(key, 2), count)]


def bell_draw(own_key, extent, width, bound, shards=(), kind=jnp.bfloat16):
    values = jax.random.normal(own_key, extent, jnp.float32) * width
    if len(shards) > 0:
        values = block_scale(own_key, extent, shards, -0.22, 0.18) * values
    return jnp.clip(values, min=-bound, max=bound).astype(kind)


def setup_inputs(seed: int = 0) -> dict:
    splits = jax.random.split(jax.random.key(seed), 8)
    return {
        "x_in": draw_x_in(jax.random.fold_in(splits[7], 71), 0),
        "norm_gain": jnp.clip(1.0 + 0.18 * jax.random.normal(splits[1], (LAYER_COUNT, MODEL_DIM), jnp.float32), 0.099609375, 1.8984375).astype(jnp.bfloat16),
        "w_query": draw_w_query(jax.random.fold_in(splits[7], 71), 0),
        "w_key": draw_w_key(jax.random.fold_in(splits[7], 71), 0),
        "value_projection": bell_draw(splits[4], (LAYER_COUNT, MODEL_DIM, KEY_VALUE_HEADS * HEAD_SIZE), MODEL_DIM ** -0.5, 0.125, ((0, 8), (1, 16), (2, 2))),
        "w_out": bell_draw(splits[5], (LAYER_COUNT, QUERY_HEADS * HEAD_SIZE, MODEL_DIM), (QUERY_HEADS * HEAD_SIZE) ** -0.5, 0.125, ((0, 8), (1, 2), (2, 16))),
        "doc_ids": jax.vmap(lambda own: jnp.searchsorted(jnp.cumsum(uneven_parts(own, max(NBLK // 4, 1), NBLK, min(6, NBLK - max(NBLK // 4, 1) + 1), 0)), jnp.arange(NBLK), side="right"))(jax.random.split(splits[6], MICRO)).reshape((MICRO, NBLK)).astype(jnp.int32),
    }


query_scale = 168.0 ** (-0.5)
rope_base = 10000.0

def rms_normed(hidden, gain_row):
    widened = hidden.astype(jnp.float32)
    mean_square = lax.optimization_barrier(jnp.mean(widened * widened, axis=-1, keepdims=True))
    return (widened * lax.rsqrt(mean_square + 1e-06) * gain_row.astype(jnp.float32)).astype(jnp.bfloat16)

def rotary_apply(tensor, token_position):
    half_dim = tensor.shape[-1] // 2
    frequency = rope_base ** (-(jnp.arange(half_dim, dtype=jnp.float32) * 2.0) / tensor.shape[-1])
    angles = token_position.astype(jnp.float32)[:, None] * frequency[None, :]
    cosine_table = jnp.cos(angles)[:, None, :]
    sine_table = jnp.sin(angles)[:, None, :]
    first_half = tensor[..., :half_dim]
    second_half = tensor[..., half_dim:]
    return jnp.concatenate([first_half * cosine_table - second_half * sine_table, second_half * cosine_table + first_half * sine_table], axis=-1)

def doc_lookup(ids_row, token_index, block):
    block_count = ids_row.shape[0]
    start_block = lax.optimization_barrier(jnp.sum((ids_row[None, :] < ids_row[:, None]).astype(jnp.int32), axis=1))
    block_of = jnp.clip(token_index // block, 0, block_count - 1)
    onehot = (block_of[:, None] == jnp.arange(block_count, dtype=jnp.int32)[None, :]).astype(jnp.int32)
    start_of = lax.optimization_barrier(jnp.sum(onehot * start_block[None, :], axis=1))
    doc_of = lax.optimization_barrier(jnp.sum(onehot * ids_row[None, :], axis=1))
    return (token_index - start_of * block, doc_of)

def attention_rows(grouped_heads, key_matrix_rows, value_rows, query_index, query_doc, key_index, key_doc):
    scores = jnp.einsum('qgrd,kgd->grqk', grouped_heads.astype(jnp.float32), key_matrix_rows.astype(jnp.float32)) * query_scale
    allowed = (key_index[None, :] >= 0) & (key_index[None, :] <= query_index[:, None])
    allowed = allowed & (query_index[:, None] - key_index[None, :] < WINDOW) & (key_doc[None, :] == query_doc[:, None])
    scores = jnp.where(allowed[None, None], scores, -1e+30)
    peak_score = lax.optimization_barrier(jnp.max(scores, axis=-1, keepdims=True))
    raised = jnp.exp(scores - peak_score)
    weights = (raised / lax.optimization_barrier(jnp.sum(raised, axis=-1, keepdims=True))).astype(jnp.bfloat16)
    layer_result = jnp.einsum('grqk,kgd->qgrd', weights.astype(jnp.float32), value_rows.astype(jnp.float32))
    return layer_result.astype(jnp.bfloat16).reshape(grouped_heads.shape[0], -1)

def one_layer(hidden, gain_row, query_weight, key_matrix, value_matrix, out_weight, ids_row):
    normalized_input = rms_normed(hidden, gain_row)
    token_index = jnp.arange(PACKED_TOKENS, dtype=jnp.int32)
    token_position, doc_of = doc_lookup(ids_row, token_index, BLOCK)
    query_matrix_rows = rotary_apply(jnp.dot(normalized_input, query_weight, preferred_element_type=jnp.float32).reshape(PACKED_TOKENS, QUERY_HEADS, HEAD_SIZE), token_position).astype(jnp.bfloat16)
    key_matrix_rows = rotary_apply(jnp.dot(normalized_input, key_matrix, preferred_element_type=jnp.float32).reshape(PACKED_TOKENS, KEY_VALUE_HEADS, HEAD_SIZE), token_position).astype(jnp.bfloat16)
    value_rows = jnp.dot(normalized_input, value_matrix, preferred_element_type=jnp.float32).astype(jnp.bfloat16).reshape(PACKED_TOKENS, KEY_VALUE_HEADS, HEAD_SIZE)
    grouped_heads = query_matrix_rows.reshape(PACKED_TOKENS, KEY_VALUE_HEADS, QUERY_HEADS // KEY_VALUE_HEADS, HEAD_SIZE)

    def block_rows(row_start):
        query_block = lax.dynamic_slice_in_dim(grouped_heads, row_start, TOK_DEV, 0)
        query_index = row_start + jnp.arange(TOK_DEV, dtype=jnp.int32)
        query_doc = lax.dynamic_slice_in_dim(doc_of, row_start, TOK_DEV, 0)
        return attention_rows(query_block, key_matrix_rows, value_rows, query_index, query_doc, token_index, doc_of)
    starts = jnp.arange(PACKED_TOKENS // TOK_DEV, dtype=jnp.int32) * TOK_DEV
    attended = lax.map(block_rows, starts).reshape(PACKED_TOKENS, QUERY_HEADS * HEAD_SIZE)
    mixed_rows = jnp.dot(attended, out_weight, preferred_element_type=jnp.float32)
    return (hidden.astype(jnp.float32) + mixed_rows).astype(jnp.bfloat16)

def reference(x_in, norm_gain, w_query, w_key, value_projection, w_out, doc_ids):
    per_layer = [[None] * MICRO for layer_num in range(LAYER_COUNT)]
    for micro_num in range(MICRO):
        hidden = x_in[micro_num]
        for layer_num in range(LAYER_COUNT):
            hidden = one_layer(hidden, norm_gain[layer_num], w_query[layer_num], w_key[layer_num], value_projection[layer_num], w_out[layer_num], doc_ids[micro_num])
            per_layer[layer_num][micro_num] = hidden
    return jnp.stack([jnp.stack(row_list) for row_list in per_layer])
```

```python
import functools
import math

import jax
import jax.numpy as jnp
from jax import lax
from jax.experimental import pallas as pl
from jax.experimental.pallas import tpu as pltpu
from jax.sharding import PartitionSpec as P

HEAD = 128
WINDOW = 1024
BLOCK = 128
HALO = 5
CHUNK = 384
QUERY_SCALE = 168.0 ** (-0.5) * math.log2(math.e)
ROPE_BASE = 10000.0
MESH = pl.DeviceIdType.MESH


def dot32(a, b):
    return jnp.dot(a, b, preferred_element_type=jnp.float32)


def columns(j):
    return pl.ds(pl.multiple_of(j * CHUNK, 128), CHUNK)


def rope(rows, cosine, sine):
    return rows * cosine + pltpu.roll(rows, HEAD // 2, 1) * sine


def kernel(
    x_ref,
    gain_ref,
    wq_ref,
    wk_ref,
    wv_ref,
    wo_ref,
    cos_ref,
    sin_ref,
    bias_ref,
    out_ref,
    hid,
    hout,
    acc,
    squares,
    qbuf,
    kv,
    att,
    own,
    part_out,
    part_in,
    z_send,
    z_recv,
    g_send,
    g_recv,
    p_send,
    p_recv,
    k_send,
    k_recv,
    io_sem,
):
    section, ctx, tp = (lax.axis_index(a) for a in ("section", "ctx", "tp"))
    sections, ctxs = lax.axis_size("section"), lax.axis_size("ctx")
    micros, _, rows, width = hid.shape
    chunks = width // CHUNK
    odd = lax.rem(ctx, 2)
    even = odd == 0
    first, last = section == 0, section == sections - 1
    partner = {"tp": 1 - tp}
    core_mate = {"ctx": ctx + 1 - 2 * odd}

    def ctx_at(by):
        return {"ctx": lax.rem(ctx + by + ctxs, ctxs)}

    def section_at(by):
        return {"section": lax.rem(section + by + sections, sections)}

    def remote(src, dst, send, recv, to):
        return pltpu.make_async_remote_copy(
            src_ref=src, dst_ref=dst, send_sem=send, recv_sem=recv, device_id=to, device_id_type=MESH
        )

    for slot in range(HALO):

        @pl.when(2 * ctx + slot < HALO)
        def _():
            for m in range(micros):
                kv[m, slot] = jnp.zeros(kv.shape[2:], kv.dtype)

    barrier = pltpu.get_barrier_semaphore()
    greeted = [partner, core_mate, section_at(1), section_at(-1)]
    greeted += [ctx_at(by) for by in (2, -2, 3, -3)]
    for peer in greeted:
        pl.semaphore_signal(barrier, inc=1, device_id=peer, device_id_type=MESH)
    pl.semaphore_wait(barrier, len(greeted))

    def z_copy(m, j):
        c = columns(j)
        return remote(
            hout.at[m, :, c], hid.at[m, tp, :, c], z_send.at[m, j], z_recv.at[m, j], section_at(1)
        )

    def gather_copy(m, j):
        here = hid.at[m, tp, :, columns(j)]
        return remote(here, here, g_send.at[m, j], g_recv.at[m, j], partner)

    def part_copy(m, j):
        c = columns(j)
        return remote(
            part_out.at[m, :, c], part_in.at[m, :, c], p_send.at[m, j], p_recv.at[m, j], partner
        )

    def halo_two(m):
        return remote(
            kv.at[m, pl.ds(5, 2)], kv.at[m, pl.ds(1, 2)], k_send.at[m, 0], k_recv.at[m, 0], ctx_at(2)
        )

    def halo_three(m):
        return remote(kv.at[m, 6], kv.at[m, 0], k_send.at[m, 1], k_recv.at[m, 1], ctx_at(3))

    def halo_mate(m):
        return remote(
            kv.at[m, pl.ds(5, 2)], kv.at[m, pl.ds(3, 2)], k_send.at[m, 2], k_recv.at[m, 2], core_mate
        )

    def pass_pair(m):
        return remote(
            kv.at[m, pl.ds(1, 2)], kv.at[m, pl.ds(3, 2)], k_send.at[m, 2], k_recv.at[m, 2], core_mate
        )

    def pass_one(m):
        return remote(kv.at[m, 2], kv.at[m, 0], k_send.at[m, 1], k_recv.at[m, 1], core_mate)

    has_two = ctx >= 2
    sends_two = ctx < ctxs - 2
    sends_three = jnp.logical_and(odd == 1, ctx < ctxs - 3)
    passes_pair = jnp.logical_and(odd == 1, has_two)
    passes_one = jnp.logical_and(even, has_two)
    gets_pair = jnp.logical_or(odd == 1, has_two)
    gets_one = ctx >= 3

    def accumulate(m, j):
        c = columns(j)
        wide = hid[m, :, :, c].reshape(2 * rows, CHUNK).astype(jnp.float32)
        squares[...] += jnp.broadcast_to(
            jnp.sum(wide * wide, axis=1, keepdims=True), squares.shape
        )
        scaled = (wide * gain_ref[:, c].astype(jnp.float32)).astype(jnp.bfloat16)
        at = 0
        for weight in (wk_ref, wv_ref, wq_ref):
            for n in range(0, weight.shape[1], 512):
                acc[:, at : at + 512] += dot32(scaled, weight[c, n : n + 512])
                at += 512

    def micro(m, carry):
        acc[...] = jnp.zeros_like(acc)
        squares[...] = jnp.zeros_like(squares)

        @pl.when(first)
        def _():
            load = pltpu.make_async_copy(x_ref.at[m], hid.at[m, tp], io_sem)
            load.start()
            load.wait()

        def arrive(j, c):
            @pl.when(jnp.logical_not(first))
            def _():
                z_copy(m, j).wait_recv()

            gather_copy(m, j).start()

            @pl.when(j > 0)
            def _():
                gather_copy(m, j - 1).wait_recv()
                accumulate(m, j - 1)

            return c

        lax.fori_loop(0, chunks, arrive, 0)
        gather_copy(m, chunks - 1).wait_recv()
        accumulate(m, chunks - 1)

        scale = lax.rsqrt(squares[...] * (1.0 / width) + 1e-06)
        cosine, sine = cos_ref[m], sin_ref[m]
        kv_heads, query_heads = kv.shape[3], qbuf.shape[1]
        for h in range(kv_heads):
            key = rope(acc[:, h * HEAD : (h + 1) * HEAD] * scale, cosine, sine)
            at = (kv_heads + h) * HEAD
            value = acc[:, at : at + HEAD] * scale
            for t in range(2):
                kv[m, 5 + t, 0, h] = key[t * rows : (t + 1) * rows].astype(jnp.bfloat16)
                kv[m, 5 + t, 1, h] = value[t * rows : (t + 1) * rows].astype(jnp.bfloat16)

        @pl.when(sends_two)
        def _():
            halo_two(m).start()

        @pl.when(sends_three)
        def _():
            halo_three(m).start()

        @pl.when(even)
        def _():
            halo_mate(m).start()

        for h in range(query_heads):
            at = (2 * kv_heads + h) * HEAD
            query = rope(acc[:, at : at + HEAD] * (scale * QUERY_SCALE), cosine, sine)
            for t in range(2):
                qbuf[t, h] = query[t * rows : (t + 1) * rows].astype(jnp.bfloat16)

        @pl.when(has_two)
        def _():
            halo_two(m).wait_recv()

        @pl.when(passes_pair)
        def _():
            pass_pair(m).start()

        @pl.when(passes_one)
        def _():
            pass_one(m).start()

        @pl.when(gets_one)
        def _():
            halo_three(m).wait_recv()

        @pl.when(gets_pair)
        def _():
            halo_mate(m).wait_recv()

        group = query_heads // kv_heads

        def attend(i, c):
            t, g = i // kv_heads, lax.rem(i, kv_heads)
            query = qbuf[t, pl.ds(g * group, group)].reshape(group * rows, HEAD)
            key = kv[m, pl.ds(t, HALO + 1), 0, g].reshape((HALO + 1) * rows, HEAD)
            value = kv[m, pl.ds(t, HALO + 1), 1, g].reshape((HALO + 1) * rows, HEAD)
            scores = lax.dot_general(
                query, key, (((1,), (1,)), ((), ())), preferred_element_type=jnp.float32
            )
            bias = bias_ref[m, t]
            for r in range(group):
                own_scores = scores[r * rows : (r + 1) * rows] + bias
                peak = jnp.max(own_scores, axis=1, keepdims=True)
                raised = jnp.exp2(own_scores - peak)
                total = jnp.sum(raised, axis=1, keepdims=True)
                mixed = dot32(raised.astype(jnp.bfloat16), value) / total
                att[t, g, :, r * HEAD : (r + 1) * HEAD] = mixed.astype(jnp.bfloat16)
            return c

        lax.fori_loop(0, 2 * kv_heads, attend, 0)

        def project(j, c):
            cols = columns(j)
            total = jnp.zeros((2 * rows, CHUNK), jnp.float32)
            for g in range(kv_heads):
                depth = group * HEAD
                total += dot32(
                    att[:, g].reshape(2 * rows, depth), wo_ref[g * depth : (g + 1) * depth, cols]
                )
            top, bottom = total[:rows], total[rows:]
            part_out[m, :, cols] = jnp.where(tp == 0, bottom, top).astype(jnp.bfloat16)
            part_copy(m, j).start()
            own[:, cols] = jnp.where(tp == 0, top, bottom) + hid[m, tp, :, cols].astype(jnp.float32)
            return c

        lax.fori_loop(0, chunks, project, 0)

        def finish(j, c):
            cols = columns(j)
            part_copy(m, j).wait_recv()
            hout[m, :, cols] = (own[:, cols] + part_in[m, :, cols].astype(jnp.float32)).astype(
                jnp.bfloat16
            )

            @pl.when(jnp.logical_not(last))
            def _():
                z_copy(m, j).start()

            return c

        lax.fori_loop(0, chunks, finish, 0)
        pltpu.make_async_copy(hout.at[m], out_ref.at[0, m], io_sem).start()
        pltpu.make_async_copy(hout.at[m], out_ref.at[0, m], io_sem).wait()
        return carry

    lax.fori_loop(0, micros, micro, 0)

    def drain(m, carry):
        def one(j, c):
            gather_copy(m, j).wait_send()
            part_copy(m, j).wait_send()

            @pl.when(jnp.logical_not(last))
            def _():
                z_copy(m, j).wait_send()

            return c

        lax.fori_loop(0, chunks, one, 0)

        @pl.when(sends_two)
        def _():
            halo_two(m).wait_send()

        @pl.when(sends_three)
        def _():
            halo_three(m).wait_send()

        @pl.when(passes_one)
        def _():
            pass_one(m).wait_send()

        @pl.when(even)
        def _():
            halo_mate(m).wait_send()

        @pl.when(passes_pair)
        def _():
            pass_pair(m).wait_send()

        return carry

    lax.fori_loop(0, micros, drain, 0)


def doc_lookup(ids, token_index):
    blocks = ids.shape[1]
    start = jnp.sum((ids[:, None, :] < ids[:, :, None]).astype(jnp.int32), axis=2)
    block_of = jnp.clip(token_index // BLOCK, 0, blocks - 1)
    onehot = (block_of[:, None] == jnp.arange(blocks, dtype=jnp.int32)[None, :]).astype(jnp.int32)
    start_of = jnp.sum(onehot[None] * start[:, None, :], axis=2)
    doc_of = jnp.sum(onehot[None] * ids[:, None, :], axis=2)
    return token_index[None] - start_of * BLOCK, doc_of


def tables(doc_ids, rows):
    ctx = lax.axis_index("ctx")
    token_index = ctx * 2 * rows + jnp.arange(2 * rows, dtype=jnp.int32)
    position, query_doc = doc_lookup(doc_ids, token_index)
    frequency = ROPE_BASE ** (-(jnp.arange(HEAD // 2, dtype=jnp.float32) * 2.0) / HEAD)
    angles = position.astype(jnp.float32)[:, :, None] * frequency
    cosine, sine = jnp.cos(angles), jnp.sin(angles)
    key_index = (2 * ctx - HALO) * rows + jnp.arange((HALO + 2) * rows, dtype=jnp.int32)
    unused, key_doc = doc_lookup(doc_ids, key_index)
    biases = []
    for t in range(2):
        q_at = token_index[t * rows : (t + 1) * rows][:, None]
        k_at = key_index[t * rows : (t + HALO + 1) * rows][None, :]
        q_doc = query_doc[:, t * rows : (t + 1) * rows, None]
        k_doc = key_doc[:, None, t * rows : (t + HALO + 1) * rows]
        allowed = (k_at >= 0) & (k_at <= q_at) & (q_at - k_at < WINDOW)
        biases.append(jnp.where(allowed[None] & (q_doc == k_doc), 0.0, -1e30))
    return (
        jnp.concatenate([cosine, cosine], axis=-1),
        jnp.concatenate([-sine, sine], axis=-1),
        jnp.stack(biases, axis=1).astype(jnp.float32),
    )


def local(x_in, norm_gain, w_query, w_key, value_projection, w_out, doc_ids):
    micros, rows, width = x_in.shape
    wq = w_query[0]
    wk = lax.all_gather(w_key, "ctx", axis=1, tiled=True)[0]
    wv = lax.all_gather(value_projection, "ctx", axis=1, tiled=True)[0]
    wo = lax.all_gather(w_out, "ctx", axis=2, tiled=True)[0]
    cosine, sine, bias = tables(doc_ids, rows)
    query_heads, kv_heads = wq.shape[1] // HEAD, wk.shape[1] // HEAD
    chunks = width // CHUNK
    vmem = pl.BlockSpec(memory_space=pltpu.VMEM)
    hbm = pl.BlockSpec(memory_space=pl.ANY)
    per_chunk = pltpu.SemaphoreType.DMA((micros, chunks))
    return pl.pallas_call(
        kernel,
        out_shape=jax.ShapeDtypeStruct((1, micros, rows, width), jnp.bfloat16),
        in_specs=[hbm] + [vmem] * 8,
        out_specs=hbm,
        scratch_shapes=[
            pltpu.VMEM((micros, 2, rows, width), jnp.bfloat16),
            pltpu.VMEM((micros, rows, width), jnp.bfloat16),
            pltpu.VMEM((2 * rows, (query_heads + 2 * kv_heads) * HEAD), jnp.float32),
            pltpu.VMEM((2 * rows, HEAD), jnp.float32),
            pltpu.VMEM((2, query_heads, rows, HEAD), jnp.bfloat16),
            pltpu.VMEM((micros, HALO + 2, 2, kv_heads, rows, HEAD), jnp.bfloat16),
            pltpu.VMEM((2, kv_heads, rows, query_heads // kv_heads * HEAD), jnp.bfloat16),
            pltpu.VMEM((rows, width), jnp.float32),
            pltpu.VMEM((micros, rows, width), jnp.bfloat16),
            pltpu.VMEM((micros, rows, width), jnp.bfloat16),
        ]
        + [per_chunk] * 6
        + [
            pltpu.SemaphoreType.DMA((micros, 3)),
            pltpu.SemaphoreType.DMA((micros, 3)),
            pltpu.SemaphoreType.DMA,
        ],
        compiler_params=pltpu.CompilerParams(
            collective_id=0, has_side_effects=True, vmem_limit_bytes=60 * 1024 * 1024
        ),
    )(x_in, norm_gain, wq, wk, wv, wo, cosine, sine, bias)


def solution(mesh):
    in_specs = (
        P(None, ("ctx", "tp"), None),
        P("section", None),
        P("section", None, "tp"),
        P("section", "ctx", "tp"),
        P("section", "ctx", "tp"),
        P("section", "tp", "ctx"),
        P(),
    )
    out_specs = P("section", None, ("ctx", "tp"), None)
    return jax.shard_map(local, mesh=mesh, in_specs=in_specs, out_specs=out_specs, check_vma=False)
```

```python
import functools
import math

import jax
import jax.numpy as jnp
from jax import lax
from jax.experimental import pallas as pl
from jax.experimental.pallas import tpu as pltpu
from jax.sharding import PartitionSpec as P

HEAD = 128
WINDOW = 1024
BLOCK = 128
HALO = 5
CHUNK = 384
PIECE = 128
QUERY_SCALE = 168.0 ** (-0.5) * math.log2(math.e)
ROPE_BASE = 10000.0
MESH = pl.DeviceIdType.MESH


def dot32(a, b):
    return jnp.dot(a, b, preferred_element_type=jnp.float32)


def columns(j):
    return pl.ds(pl.multiple_of(j * CHUNK, 128), CHUNK)


def rope(rows, cosine, sine):
    return rows * cosine + pltpu.roll(rows, HEAD // 2, 1) * sine


def kernel(
    x_ref,
    gain_ref,
    wq_ref,
    wk_ref,
    wv_ref,
    wo_ref,
    cos_ref,
    sin_ref,
    bias_ref,
    out_ref,
    wq,
    kv_parts,
    o_parts,
    wkv,
    wo,
    hid,
    hout,
    acc,
    squares,
    qbuf,
    kv,
    att,
    own,
    part_out,
    part_in,
    z_send,
    z_recv,
    g_send,
    g_recv,
    p_send,
    p_recv,
    k_send,
    k_recv,
    w_send,
    w_recv,
    load_sem,
    io_sem,
):
    section, ctx, tp = (lax.axis_index(a) for a in ("section", "ctx", "tp"))
    sections, ctxs = lax.axis_size("section"), lax.axis_size("ctx")
    micros, _, rows, width = hid.shape
    chunks, per_chunk = width // CHUNK, CHUNK // PIECE
    kv_heads, query_heads = kv.shape[1], qbuf.shape[1]
    group = query_heads // kv_heads
    odd = lax.rem(ctx, 2)
    even = odd == 0
    first, last = section == 0, section == sections - 1
    partner = {"tp": 1 - tp}
    mate = ctx + 1 - 2 * odd
    core_mate = {"ctx": mate}

    def wrap(index):
        return lax.rem(index + ctxs, ctxs)

    def ctx_at(by):
        return {"ctx": wrap(ctx + by)}

    def section_at(by):
        return {"section": lax.rem(section + by + sections, sections)}

    def remote(src, dst, send, recv, to):
        return pltpu.make_async_remote_copy(
            src_ref=src, dst_ref=dst, send_sem=send, recv_sem=recv, device_id=to, device_id_type=MESH
        )

    half = wo_ref.shape[1] // 2
    loads = [
        pltpu.make_async_copy(wk_ref.at[0], kv_parts.at[0, ctx], load_sem.at[0]),
        pltpu.make_async_copy(wv_ref.at[0], kv_parts.at[1, ctx], load_sem.at[1]),
        pltpu.make_async_copy(wo_ref.at[0, pl.ds(0, half)], o_parts.at[0, ctx], load_sem.at[2]),
        pltpu.make_async_copy(wo_ref.at[0, pl.ds(half, half)], o_parts.at[1, ctx], load_sem.at[3]),
        pltpu.make_async_copy(wq_ref.at[0], wq, load_sem.at[4]),
    ]
    for load in loads:
        load.start()

    def x_load(m):
        return pltpu.make_async_copy(x_ref.at[m], hid.at[m, tp], io_sem.at[m])

    @pl.when(first)
    def _():
        for m in range(micros):
            x_load(m).start()

    for slot in range(HALO):

        @pl.when(2 * ctx + slot < HALO)
        def _():
            for m in range(micros):
                for g in range(kv_heads):
                    kv[m, g, slot] = jnp.zeros(kv.shape[3:], kv.dtype)

    barrier = pltpu.get_barrier_semaphore()
    greeted = [partner, core_mate, section_at(1), section_at(-1)]
    greeted += [ctx_at(by) for by in (2, -2, 3, -3, 4, -4)]
    for peer in greeted:
        pl.semaphore_signal(barrier, inc=1, device_id=peer, device_id_type=MESH)
    pl.semaphore_wait(barrier, len(greeted))

    def piece(j):
        return pl.ds(pl.multiple_of(j * PIECE, PIECE), PIECE)

    def z_copy(m, j):
        c = piece(j)
        return remote(
            hout.at[m, :, c], hid.at[m, tp, :, c], z_send.at[m, j], z_recv.at[m, j], section_at(1)
        )

    def gather_copy(m, j):
        here = hid.at[m, tp, :, piece(j)]
        return remote(here, here, g_send.at[m, j], g_recv.at[m, j], partner)

    def part_copy(m, j):
        c = piece(j)
        return remote(
            part_out.at[m, :, c], part_in.at[m, :, c], p_send.at[m, j], p_recv.at[m, j], partner
        )

    def halo(m, g, n, src, dst, to):
        return remote(
            kv.at[m, g, src], kv.at[m, g, dst], k_send.at[m, n, g], k_recv.at[m, n, g], to
        )

    def halo_two(m, g):
        return halo(m, g, 0, pl.ds(5, 2), pl.ds(1, 2), ctx_at(2))

    def halo_three(m, g):
        return halo(m, g, 1, 6, 0, ctx_at(3))

    def halo_mate(m, g):
        return halo(m, g, 2, pl.ds(5, 2), pl.ds(3, 2), core_mate)

    def pass_pair(m, g):
        return halo(m, g, 2, pl.ds(1, 2), pl.ds(3, 2), core_mate)

    def pass_one(m, g):
        return halo(m, g, 1, 2, 0, core_mate)

    has_two = ctx >= 2
    sends_two = ctx < ctxs - 2
    sends_three = jnp.logical_and(odd == 1, ctx < ctxs - 3)
    passes_pair = jnp.logical_and(odd == 1, has_two)
    passes_one = jnp.logical_and(even, has_two)
    gets_pair = jnp.logical_or(odd == 1, has_two)
    gets_one = ctx >= 3

    across = ctx + 2 - 4 * lax.rem(ctx // 2, 2)
    stream = [wrap(at + by) for by in (0, -4, 4, 8) for at in (ctx, across)]
    mine, beside, up, up_beside, down, down_beside, far, far_beside = stream
    to_across, to_down, to_up = {"ctx": across}, ctx_at(4), ctx_at(-4)

    def w_copy(kind, p, slot, n, to):
        ref = (kv_parts, o_parts)[kind].at[p, slot]
        k = 2 * kind + p
        return remote(ref, ref, w_send.at[k, n], w_recv.at[k, slot], to)

    def w_wait(kind, p, slot):
        w_copy(kind, p, slot, 0, core_mate).wait_recv()

    def w_own(kind):
        for p in range(2):
            for n, to in enumerate((to_across, to_down, to_up, core_mate)):
                w_copy(kind, p, mine, n, to).start()

    def w_beside(kind):
        for p in range(2):
            w_wait(kind, p, beside)
            for n, to in enumerate((to_down, to_up, core_mate)):
                w_copy(kind, p, beside, 4 + n, to).start()

    def w_onward(kind):
        for p, onward in enumerate((to_down, to_up)):
            for n, slot in enumerate(((up, up_beside), (down, down_beside))[p]):
                w_wait(kind, p, slot)
                w_copy(kind, p, slot, 7 + n, onward).start()
                w_copy(kind, p, slot, 9 + n, core_mate).start()
        for p in range(2):
            for n, slot in enumerate(((down, down_beside), (up, up_beside))[p]):
                w_wait(kind, p, slot)
                w_copy(kind, p, slot, 11 + n, core_mate).start()

    def w_last(kind):
        for p in range(2):
            for n, slot in enumerate((far, far_beside)):
                w_wait(kind, p, slot)
                w_copy(kind, p, slot, 13 + n, core_mate).start()
        for p in range(2):
            for slot in stream:
                w_wait(kind, p, slot + 1 - 2 * odd)

    def w_drain(kind):
        for p in range(2):
            for n in range(15):
                w_copy(kind, p, mine, n, core_mate).wait_send()

    deep = kv_parts.shape[2]

    def assemble_kv():
        for p in range(2):
            for i in range(kv_parts.shape[1]):
                wkv[p, i * deep : (i + 1) * deep, :] = kv_parts[p, i]

    def assemble_o():
        step = 32

        def some(r, c):
            for p in range(2):
                at = pl.ds(pl.multiple_of(r * step, step), step)
                to = pl.ds(pl.multiple_of(p * half + r * step, step), step)
                for i in range(o_parts.shape[1]):
                    wo[to, i * deep : (i + 1) * deep] = o_parts[p, i, at, :]
            return c

        lax.fori_loop(0, half // step, some, 0)

    for load in loads[:4]:
        load.wait()
    w_own(0)

    @pl.when(first)
    def _():
        for m in range(micros):
            x_load(m).wait()

        def spread(i, c):
            gather_copy(i // (chunks * per_chunk), lax.rem(i, chunks * per_chunk)).start()
            return c

        lax.fori_loop(0, micros * chunks * per_chunk, spread, 0)

    w_beside(0)
    w_onward(0)
    w_last(0)
    w_own(1)
    assemble_kv()

    @pl.when(jnp.logical_not(first))
    def _():
        w_beside(1)
        w_onward(1)
        w_last(1)
        assemble_o()

    loads[4].wait()

    def accumulate(m, j):
        c = columns(j)
        wide = hid[m, :, :, c].reshape(2 * rows, CHUNK).astype(jnp.float32)
        squares[...] += jnp.broadcast_to(
            jnp.sum(wide * wide, axis=1, keepdims=True), squares.shape
        )
        scaled = (wide * gain_ref[:, c].astype(jnp.float32)).astype(jnp.bfloat16)
        at = 0
        for weight in (wkv.at[0], wkv.at[1], wq):
            for n in range(0, weight.shape[1], 512):
                acc[:, at : at + 512] += dot32(scaled, weight[c, n : n + 512])
                at += 512

    def micro(m, carry):
        acc[...] = jnp.zeros_like(acc)
        squares[...] = jnp.zeros_like(squares)
        starts = jnp.logical_and(first, m == 0)

        def gathered(j):
            for i in range(per_chunk):
                gather_copy(m, j * per_chunk + i).wait_recv()

        def arrive(j, c):
            @pl.when(jnp.logical_not(first))
            def _():
                for i in range(per_chunk):
                    z_copy(m, j * per_chunk + i).wait_recv()
                    gather_copy(m, j * per_chunk + i).start()

            @pl.when(j > 0)
            def _():
                gathered(j - 1)
                accumulate(m, j - 1)

            return c

        lax.fori_loop(0, chunks, arrive, 0)
        gathered(chunks - 1)
        accumulate(m, chunks - 1)

        @pl.when(starts)
        def _():
            w_beside(1)

        scale = lax.rsqrt(squares[...] * (1.0 / width) + 1e-06)
        cosine, sine = cos_ref[m], sin_ref[m]
        for h in range(kv_heads):
            key = rope(acc[:, h * HEAD : (h + 1) * HEAD] * scale, cosine, sine)
            at = (kv_heads + h) * HEAD
            value = acc[:, at : at + HEAD] * scale
            for t in range(2):
                kv[m, h, 5 + t, 0] = key[t * rows : (t + 1) * rows].astype(jnp.bfloat16)
                kv[m, h, 5 + t, 1] = value[t * rows : (t + 1) * rows].astype(jnp.bfloat16)

            @pl.when(sends_two)
            def _():
                halo_two(m, h).start()

            @pl.when(sends_three)
            def _():
                halo_three(m, h).start()

            @pl.when(even)
            def _():
                halo_mate(m, h).start()

        for h in range(query_heads):
            at = (2 * kv_heads + h) * HEAD
            query = rope(acc[:, at : at + HEAD] * (scale * QUERY_SCALE), cosine, sine)
            for t in range(2):
                qbuf[t, h] = query[t * rows : (t + 1) * rows].astype(jnp.bfloat16)

        def relay(g):
            @pl.when(has_two)
            def _():
                halo_two(m, g).wait_recv()

            @pl.when(passes_pair)
            def _():
                pass_pair(m, g).start()

            @pl.when(passes_one)
            def _():
                pass_one(m, g).start()

        def attend(g, c):
            @pl.when(g < kv_heads - 1)
            def _():
                relay(g + 1)

            @pl.when(gets_one)
            def _():
                halo_three(m, g).wait_recv()

            @pl.when(gets_pair)
            def _():
                halo_mate(m, g).wait_recv()

            for t in range(2):
                query = qbuf[t, pl.ds(g * group, group)].reshape(group * rows, HEAD)
                key = kv[m, g, t : t + HALO + 1, 0].reshape((HALO + 1) * rows, HEAD)
                value = kv[m, g, t : t + HALO + 1, 1].reshape((HALO + 1) * rows, HEAD)
                scores = lax.dot_general(
                    query, key, (((1,), (1,)), ((), ())), preferred_element_type=jnp.float32
                )
                bias = bias_ref[m, t]
                for r in range(group):
                    own_scores = scores[r * rows : (r + 1) * rows] + bias
                    peak = jnp.max(own_scores, axis=1, keepdims=True)
                    raised = jnp.exp2(own_scores - peak)
                    total = jnp.sum(raised, axis=1, keepdims=True)
                    mixed = dot32(raised.astype(jnp.bfloat16), value) / total
                    att[t, g, :, r * HEAD : (r + 1) * HEAD] = mixed.astype(jnp.bfloat16)

            @pl.when(jnp.logical_and(starts, g == 0))
            def _():
                w_onward(1)

            return c

        relay(0)
        lax.fori_loop(0, kv_heads, attend, 0)

        @pl.when(starts)
        def _():
            w_last(1)
            assemble_o()

        def project(j, c):
            cols = columns(j)
            total = jnp.zeros((2 * rows, CHUNK), jnp.float32)
            for g in range(kv_heads):
                depth = group * HEAD
                total += dot32(
                    att[:, g].reshape(2 * rows, depth), wo[g * depth : (g + 1) * depth, cols]
                )
            top, bottom = total[:rows], total[rows:]
            part_out[m, :, cols] = jnp.where(tp == 0, bottom, top).astype(jnp.bfloat16)
            for i in range(per_chunk):
                part_copy(m, j * per_chunk + i).start()
            own[:, cols] = jnp.where(tp == 0, top, bottom) + hid[m, tp, :, cols].astype(jnp.float32)
            return c

        lax.fori_loop(0, chunks, project, 0)

        def finish(j, c):
            cols = piece(j)
            part_copy(m, j).wait_recv()
            hout[m, :, cols] = (own[:, cols] + part_in[m, :, cols].astype(jnp.float32)).astype(
                jnp.bfloat16
            )

            @pl.when(jnp.logical_not(last))
            def _():
                z_copy(m, j).start()

            return c

        lax.fori_loop(0, chunks * per_chunk, finish, 0)
        pltpu.make_async_copy(hout.at[m], out_ref.at[0, m], io_sem.at[m]).start()
        return carry

    lax.fori_loop(0, micros, micro, 0)

    w_drain(0)
    w_drain(1)

    def drain(m, carry):
        pltpu.make_async_copy(hout.at[m], out_ref.at[0, m], io_sem.at[m]).wait()

        def one(j, c):
            gather_copy(m, j).wait_send()
            part_copy(m, j).wait_send()

            @pl.when(jnp.logical_not(last))
            def _():
                z_copy(m, j).wait_send()

            return c

        lax.fori_loop(0, chunks * per_chunk, one, 0)

        def heads(g, c):
            @pl.when(sends_two)
            def _():
                halo_two(m, g).wait_send()

            @pl.when(sends_three)
            def _():
                halo_three(m, g).wait_send()

            @pl.when(passes_one)
            def _():
                pass_one(m, g).wait_send()

            @pl.when(even)
            def _():
                halo_mate(m, g).wait_send()

            @pl.when(passes_pair)
            def _():
                pass_pair(m, g).wait_send()

            return c

        lax.fori_loop(0, kv_heads, heads, 0)
        return carry

    lax.fori_loop(0, micros, drain, 0)


def doc_lookup(ids, token_index):
    blocks = ids.shape[1]
    start = jnp.sum((ids[:, None, :] < ids[:, :, None]).astype(jnp.int32), axis=2)
    block_of = jnp.clip(token_index // BLOCK, 0, blocks - 1)
    onehot = (block_of[:, None] == jnp.arange(blocks, dtype=jnp.int32)[None, :]).astype(jnp.int32)
    start_of = jnp.sum(onehot[None] * start[:, None, :], axis=2)
    doc_of = jnp.sum(onehot[None] * ids[:, None, :], axis=2)
    return token_index[None] - start_of * BLOCK, doc_of


def tables(doc_ids, rows):
    ctx = lax.axis_index("ctx")
    token_index = ctx * 2 * rows + jnp.arange(2 * rows, dtype=jnp.int32)
    position, query_doc = doc_lookup(doc_ids, token_index)
    frequency = ROPE_BASE ** (-(jnp.arange(HEAD // 2, dtype=jnp.float32) * 2.0) / HEAD)
    angles = position.astype(jnp.float32)[:, :, None] * frequency
    cosine, sine = jnp.cos(angles), jnp.sin(angles)
    key_index = (2 * ctx - HALO) * rows + jnp.arange((HALO + 2) * rows, dtype=jnp.int32)
    unused, key_doc = doc_lookup(doc_ids, key_index)
    biases = []
    for t in range(2):
        q_at = token_index[t * rows : (t + 1) * rows][:, None]
        k_at = key_index[t * rows : (t + HALO + 1) * rows][None, :]
        q_doc = query_doc[:, t * rows : (t + 1) * rows, None]
        k_doc = key_doc[:, None, t * rows : (t + HALO + 1) * rows]
        allowed = (k_at >= 0) & (k_at <= q_at) & (q_at - k_at < WINDOW)
        biases.append(jnp.where(allowed[None] & (q_doc == k_doc), 0.0, -1e30))
    return (
        jnp.concatenate([cosine, cosine], axis=-1),
        jnp.concatenate([-sine, sine], axis=-1),
        jnp.stack(biases, axis=1).astype(jnp.float32),
    )


def local(x_in, norm_gain, w_query, w_key, value_projection, w_out, doc_ids):
    micros, rows, width = x_in.shape
    ctxs = lax.axis_size("ctx")
    cosine, sine, bias = tables(doc_ids, rows)
    query_cols, key_cols = w_query.shape[2], w_key.shape[2]
    deep = w_key.shape[1]
    query_heads, kv_heads = query_cols // HEAD, key_cols // HEAD
    pieces = width // PIECE
    vmem = pl.BlockSpec(memory_space=pltpu.VMEM)
    hbm = pl.BlockSpec(memory_space=pl.ANY)
    per_piece = pltpu.SemaphoreType.DMA((micros, pieces))
    per_head = pltpu.SemaphoreType.DMA((micros, 3, kv_heads))
    return pl.pallas_call(
        kernel,
        out_shape=jax.ShapeDtypeStruct((1, micros, rows, width), jnp.bfloat16),
        in_specs=[hbm, vmem] + [hbm] * 4 + [vmem] * 3,
        out_specs=hbm,
        scratch_shapes=[
            pltpu.VMEM((width, query_cols), jnp.bfloat16),
            pltpu.VMEM((2, ctxs, deep, key_cols), jnp.bfloat16),
            pltpu.VMEM((2, ctxs, query_cols // 2, deep), jnp.bfloat16),
            pltpu.VMEM((2, width, key_cols), jnp.bfloat16),
            pltpu.VMEM((query_cols, width), jnp.bfloat16),
            pltpu.VMEM((micros, 2, rows, width), jnp.bfloat16),
            pltpu.VMEM((micros, rows, width), jnp.bfloat16),
            pltpu.VMEM((2 * rows, query_cols + 2 * key_cols), jnp.float32),
            pltpu.VMEM((2 * rows, HEAD), jnp.float32),
            pltpu.VMEM((2, query_heads, rows, HEAD), jnp.bfloat16),
            pltpu.VMEM((micros, kv_heads, HALO + 2, 2, rows, HEAD), jnp.bfloat16),
            pltpu.VMEM((2, kv_heads, rows, query_heads // kv_heads * HEAD), jnp.bfloat16),
            pltpu.VMEM((rows, width), jnp.float32),
            pltpu.VMEM((micros, rows, width), jnp.bfloat16),
            pltpu.VMEM((micros, rows, width), jnp.bfloat16),
        ]
        + [per_piece] * 6
        + [per_head] * 2
        + [
            pltpu.SemaphoreType.DMA((4, 15)),
            pltpu.SemaphoreType.DMA((4, ctxs)),
            pltpu.SemaphoreType.DMA((5,)),
            pltpu.SemaphoreType.DMA((micros,)),
        ],
        compiler_params=pltpu.CompilerParams(
            collective_id=0, has_side_effects=True, vmem_limit_bytes=60 * 1024 * 1024
        ),
    )(x_in, norm_gain, w_query, w_key, value_projection, w_out, cosine, sine, bias)


def solution(mesh):
    in_specs = (
        P(None, ("ctx", "tp"), None),
        P("section", None),
        P("section", None, "tp"),
        P("section", "ctx", "tp"),
        P("section", "ctx", "tp"),
        P("section", "tp", "ctx"),
        P(),
    )
    out_specs = P("section", None, ("ctx", "tp"), None)
    return jax.shard_map(local, mesh=mesh, in_specs=in_specs, out_specs=out_specs, check_vma=False)
```
